32 devices in a mesh: field: 2 (over core), sx: 4 (over y, x), sy: 4 (over z).
Axes of the slice: x: 2, y: 2, z: 4, core: 2. Of those that a mesh axis runs over, the one named last changes fastest.
Arguments:
- inner_block: bfloat16 [4, 40, 8, 128, 128], P('field', 'sx', 'sy'), may hold values from 0.0004 to 0.03, as said below
- east_block: bfloat16 [4, 40, 8, 128, 128], P('field', 'sx', 'sy'), may hold values from 0.0004 to 0.03, as said below
- north_block: bfloat16 [4, 40, 8, 128, 128], P('field', 'sx', 'sy'), may hold values from 0.0004 to 0.03, as said below
- shift_diag: float32 [4, 40, 8, 128], P('field', 'sx', 'sy'), may hold values from 0.2 to 2
- coupling: float32 [4, 4, 40, 8, 128], P('field', None, 'sx', 'sy'), may hold values from -4 to 4
- coarse_flags: int32 [4, 40, 8, 128], P('field', 'sx', 'sy'), may hold values from 0 to 1, as said below
Outputs:
- coarse_node: bfloat16 [4, 4, 40, 8, 128, 128], P('field', None, 'sx', 'sy')
- coarse_east: bfloat16 [4, 40, 8, 128, 128], P('field', 'sx', 'sy')
- coarse_north: bfloat16 [4, 40, 8, 128, 128], P('field', 'sx', 'sy')
The draws below stay inside these ranges and needn't reach their ends.
Inputs may be any that keep to these rules, and one draw needn't show every extreme that they name: `coarse_flags`: 1 marks a coarse point of its field; the share of coarse points is drawn for each tile and field. `inner_block`: positive magnitudes. `east_block`: positive magnitudes. `north_block`: positive magnitudes.
All inputs are finite; a program needn't handle non-finite values.
Results may differ from the reference program's by a relative error of at most 0.0046.
Values may be sent and summed in bfloat16 or wider, within the bound.
No kernel may reach another device: no remote copies, remote signals or barrier semaphores. Data moves between devices by JAX's collectives and lax.ppermute only.
A program may use at most 128 MiB of HBM per device.

```python
import math
import jax
import jax.numpy as jnp
from jax import lax

M = 128
NF = 4
NTX = 40
NTY = 8


def draw_coarse_flags(key, part):
    level_key = jax.random.fold_in(key, 11)
    node_key = jax.random.fold_in(key, 12)
    levels = jax.random.randint(level_key, (NF, NTX, NTY, 1), 0, 6)
    limit = jnp.right_shift(jnp.full(levels.shape, 64, jnp.int32), levels + 1)
    draws = jax.random.randint(node_key, (NF, NTX, NTY, M), 0, 64)
    return (draws < limit).astype(jnp.int32)


def banded_magnitudes(key, salt):
    near_key = jax.random.fold_in(key, salt)
    far_key = jax.random.fold_in(key, salt + 1)
    shape = (NF, NTX, NTY, M, M)
    width = float(max(M // 16, 2))
    nodes = jnp.arange(M, dtype=jnp.float32)
    distance = jnp.abs(nodes[:, None] - nodes[None, :])
    near = jnp.exp(jax.random.uniform(near_key, shape, jnp.float32, -0.9, 0.0))
    far = jnp.exp(jax.random.uniform(far_key, shape, jnp.float32, -1.38, 0.0))
    length = width
    value = 0.0019 * far + 0.0279 * jnp.exp(-distance / length) * near
    return value.astype(jnp.bfloat16)


def draw_inner_block(key, part):
    return banded_magnitudes(key, 21)


def draw_east_block(key, part):
    return banded_magnitudes(key, 31)


def draw_north_block(key, part):
    return banded_magnitudes(key, 41)


def shard_levels(key, extent, shards, low, top_value):
    def one(position, parts):
        heights = jax.random.uniform(jax.random.fold_in(jax.random.fold_in(key, 6), position), (parts,), jnp.float32, low / len(shards), top_value / len(shards))
        return jnp.repeat(jnp.exp(heights), extent[position] // parts).reshape((-1,) + (1,) * (len(extent) - position - 1))

    loudness = one(*shards[0])
    for cut in shards[1:]:
        loudness = loudness * one(*cut)
    return loudness


def noise(own_key, dims, spread, bound, shards=(), kind=jnp.bfloat16):
    loudness = shard_levels(own_key, dims, shards, -0.22, 0.18) if shards else 1.0
    array = jax.random.normal(own_key, dims, jnp.float32) * spread * loudness
    return jnp.minimum(jnp.maximum(array, -bound), bound).astype(kind)


def setup_inputs(seed: int = 0) -> dict:
    splits = jax.random.split(jax.random.key(seed), 7)
    return {
        "inner_block": draw_inner_block(jax.random.fold_in(splits[6], 71), 0),
        "east_block": draw_east_block(jax.random.fold_in(splits[6], 71), 0),
        "north_block": draw_north_block(jax.random.fold_in(splits[6], 71), 0),
        "shift_diag": jnp.clip(jnp.exp(math.log(2.0) - 2.3025851 * jax.random.uniform(splits[3], (NF, NTX, NTY, M), jnp.float32) ** shard_levels(splits[3], (NF, NTX, NTY, M), ((0, 2), (1, 4), (2, 4)), -0.2, 0.2)), 0.2, 2.0),
        "coupling": noise(splits[4], (NF, NF, NTX, NTY, M), 1.0, 4.0, ((0, 2), (2, 4), (3, 4)), jnp.float32),
        "coarse_flags": draw_coarse_flags(jax.random.fold_in(splits[6], 71), 0),
    }


def interpolate(matrix, shift, flags):
    tile_nodes = matrix.shape[-1]
    unit = jnp.eye(tile_nodes, dtype=bool)
    offdiag = jnp.where(unit, jnp.zeros((), matrix.dtype), matrix)
    weights = offdiag.astype(jnp.float32)
    coarse = flags.astype(jnp.float32)
    row_total = jnp.sum(weights, axis=-1)
    strong = jnp.sum(weights * coarse[..., None, :], axis=-1)
    diagonal = row_total + shift
    scaling = row_total / jnp.maximum(strong, row_total / 32.0)
    factor = (1.0 - coarse) * scaling / diagonal
    result = coarse[..., :, None] * unit.astype(jnp.float32) + factor[..., :, None] * coarse[..., None, :] * weights
    return result.astype(jnp.bfloat16), offdiag, diagonal


def product(left, right):
    return jnp.einsum('xyik,xykj->xyij', left.astype(jnp.float32), right.astype(jnp.float32), precision=lax.Precision.HIGHEST)


def transposed(left, right):
    return jnp.einsum('xyia,xyib->xyab', left.astype(jnp.float32), right.astype(jnp.float32), precision=lax.Precision.HIGHEST)


def reference(inner_block, east_block, north_block, shift_diag, coupling, coarse_flags):
    all_interp = lax.map(lambda index: interpolate(inner_block[index], shift_diag[index], coarse_flags[index])[0], jnp.arange(NF, dtype=jnp.int32))

    def field_rows(row_field):
        interp, offdiag, diagonal = interpolate(inner_block[row_field], shift_diag[row_field], coarse_flags[row_field])
        own_term = diagonal[..., None] * interp.astype(jnp.float32) - product(offdiag, interp)

        def column(col_field):
            weighted = jnp.where(col_field == row_field, own_term, jnp.zeros_like(own_term))
            weighted = weighted + coupling[row_field, col_field][..., None] * all_interp[col_field].astype(jnp.float32)
            return transposed(interp, weighted.astype(jnp.bfloat16)).astype(jnp.bfloat16)

        node_rows = lax.map(column, jnp.arange(NF, dtype=jnp.int32))
        east_interp = jnp.concatenate([interp[1:], jnp.zeros_like(interp[:1])], axis=0)
        east_image = product(east_block[row_field], east_interp).astype(jnp.bfloat16)
        east_rows = (-transposed(interp, east_image)).astype(jnp.bfloat16)
        north_interp = jnp.concatenate([interp[:, 1:], jnp.zeros_like(interp[:, :1])], axis=1)
        north_image = product(north_block[row_field], north_interp).astype(jnp.bfloat16)
        north_rows = (-transposed(interp, north_image)).astype(jnp.bfloat16)
        return node_rows, east_rows, north_rows

    coarse_node, coarse_east, coarse_north = lax.map(field_rows, jnp.arange(NF, dtype=jnp.int32))
    return (coarse_node, coarse_east, coarse_north)
```

```python
import jax
import jax.numpy as jnp
from jax import lax
from jax.experimental import pallas as pl
from jax.experimental.pallas import tpu as pltpu
from jax.sharding import PartitionSpec as P

BF = jnp.bfloat16
F32 = jnp.float32
ANY = pl.BlockSpec(memory_space=pl.ANY)


def nn(left, right):
    return lax.dot_general(left, right, (((1,), (0,)), ((), ())), preferred_element_type=F32)


def nt(left, right):
    return lax.dot_general(left, right, (((1,), (1,)), ((), ())), preferred_element_type=F32)


def iota(shape, dim):
    return lax.broadcasted_iota(jnp.int32, shape, dim)


def round_up(value, step):
    return -(-value // step) * step


def one_hot(key_row, rows):
    m = key_row.shape[-1]
    hit = iota((rows, m), 0).astype(F32) == jnp.broadcast_to(key_row, (rows, m))
    return jnp.where(hit, 1.0, 0.0).astype(BF)


def interp_kernel(y_lo, y_hi, pack, shape, *refs):
    nf, nx, ny, m = shape
    tiles = [(f, x, y) for x in range(nx) for f in range(nf) for y in range(y_lo, y_hi)]
    count = len(tiles)
    half = m // 2
    if pack:
        w_hbm, s_hbm, c_hbm, p_hbm, a_hbm, z_hbm = refs[:6]
        wv, sv, cv, pv, av, fscr, cscr, insem, outsem, zv, kscr = refs[6:]
    else:
        w_hbm, s_hbm, c_hbm, _, p_hbm, a_hbm = refs[:6]
        wv, sv, cv, pv, av, fscr, cscr, insem, outsem = refs[6:]
    c_copy = pltpu.make_async_copy(c_hbm, cv, insem.at[nx])
    s_copy = pltpu.make_async_copy(s_hbm, sv, insem.at[nx + 1])
    c_copy.start()
    s_copy.start()
    w_copies = []
    for x in range(nx):
        copy = pltpu.make_async_copy(w_hbm.at[:, x, pl.ds(y_lo, y_hi - y_lo)], wv.at[x], insem.at[x])
        copy.start()
        w_copies.append(copy)
    rows = cscr.shape[0]
    cscr[...] = jnp.zeros((rows, m), F32)
    fscr[...] = jnp.zeros(fscr.shape, F32)
    eye = iota((m, m), 0) == iota((m, m), 1)
    off = jnp.where(eye, 0.0, 1.0).astype(BF)
    c_copy.wait()
    for t, (f, x, y) in enumerate(tiles):
        cscr[pl.ds(t, 1), :] = cv[f, x, pl.ds(y, 1), :].astype(F32)
    if pack:
        cs = cscr[...]
        ones = jnp.ones((m, m), BF)
        few = nn(cs.astype(BF), ones) <= half
        sel = jnp.where(few, cs, 1.0 - cs)
        before = jnp.where(iota((m, m), 0) < iota((m, m), 1), 1.0, 0.0).astype(BF)
        rank = nn(sel.astype(BF), before)
        kscr[0] = jnp.where(sel > 0.0, rank, -1.0)
        kscr[1] = jnp.where(few, 1.0, 0.0)
        z_rows = count * half
        zv[pl.ds(z_rows, rows), :] = kscr[0].astype(BF)
        zv[pl.ds(z_rows + rows, rows), :] = kscr[1].astype(BF)
        zv[pl.ds(z_rows + 2 * rows, rows), :] = cs.astype(BF)
    s_copy.wait()
    lhs_top = iota((16, m), 0) < 8
    for t, (f, x, y) in enumerate(tiles):
        if f == 0 and y == y_lo:
            w_copies[x].wait()
        c_row = cscr[pl.ds(t, 1), :]
        lhs = jnp.where(lhs_top, 1.0, jnp.broadcast_to(c_row, (16, m))).astype(BF)
        sums = nt(lhs, wv[x, f, y - y_lo] * off)
        total = sums[0:1, :]
        strong = sums[8:9, :]
        diagonal = total + sv[f, x, pl.ds(y, 1), :]
        scaling = total / jnp.maximum(strong, total / 32.0)
        fscr[pl.ds(t, 1), :] = (1.0 - c_row) * scaling / diagonal
        av[pl.ds(t, 1), :] = diagonal
    columns = jnp.transpose(fscr[...])
    copies = []
    for t, (f, x, y) in enumerate(tiles):
        c_row = cscr[pl.ds(t, 1), :]
        scaled = (wv[x, f, y - y_lo].astype(F32) * c_row) * columns[:, t : t + 1]
        value = jnp.where(eye, jnp.broadcast_to(c_row, (m, m)), scaled)
        pv[x, f, y - y_lo] = value.astype(BF)
        if pack:
            picked = jnp.where(
                jnp.broadcast_to(kscr[1, pl.ds(t, 1), :], (m, m)) > 0.5, jnp.transpose(value), value
            ).astype(BF)
            zv[pl.ds(t * half, half), :] = nn(one_hot(kscr[0, pl.ds(t, 1), :], half), picked).astype(BF)
        if f == nf - 1 and y == y_hi - 1:
            copy = pltpu.make_async_copy(
                pv.at[x], p_hbm.at[:, x, pl.ds(y_lo, y_hi - y_lo)], outsem.at[x]
            )
            copy.start()
            copies.append(copy)
    copy = pltpu.make_async_copy(av, a_hbm, outsem.at[nx])
    copy.start()
    copies.append(copy)
    if pack:
        copy = pltpu.make_async_copy(zv, z_hbm, outsem.at[nx + 1])
        copy.start()
        copies.append(copy)
    for copy in copies:
        copy.wait()


def interp_call(inner, shift, flags, partial, y_lo, y_hi):
    nf, nx, ny, m, _ = inner.shape
    pack = partial is None
    span = y_hi - y_lo
    count = nf * nx * span
    rows = round_up(count, 16)
    p_shape = jax.ShapeDtypeStruct(inner.shape, BF)
    a_shape = jax.ShapeDtypeStruct((rows, m), F32)
    out_shape = [p_shape, a_shape]
    scratch = [
        pltpu.VMEM((nx, nf, span, m, m), BF),
        pltpu.VMEM(shift.shape, F32),
        pltpu.VMEM(flags.shape, jnp.int32),
        pltpu.VMEM((nx, nf, span, m, m), BF),
        pltpu.VMEM((rows, m), F32),
        pltpu.VMEM((round_up(rows, m), m), F32),
        pltpu.VMEM((rows, m), F32),
        pltpu.SemaphoreType.DMA((nx + 2,)),
        pltpu.SemaphoreType.DMA((nx + 2,)),
    ]
    operands = [inner, shift, flags]
    aliases = {}
    if pack:
        z_rows = count * (m // 2) + 3 * rows
        out_shape.append(jax.ShapeDtypeStruct((z_rows, m), BF))
        scratch += [pltpu.VMEM((z_rows, m), BF), pltpu.VMEM((2, rows, m), F32)]
    else:
        operands.append(partial)
        aliases = {3: 0}

    def kernel(*refs):
        interp_kernel(y_lo, y_hi, pack, (nf, nx, ny, m), *refs)

    return pl.pallas_call(
        kernel,
        out_shape=out_shape,
        in_specs=[ANY] * len(operands),
        out_specs=[ANY] * len(out_shape),
        scratch_shapes=scratch,
        input_output_aliases=aliases,
        name="interp_pack" if pack else "interp_rest",
    )(*operands)


def main_kernel(shape, groups, *refs):
    nf, nx, ny, m = shape
    w_hbm, e_hbm, n_hbm, p_hbm, d_hbm, a0_hbm, a1_hbm = refs[:7]
    q_hbm = refs[7 : 6 + groups]
    refs = refs[6 + groups :]
    node_hbm, east_hbm, north_hbm, ge_hbm, gn_hbm = refs[:5]
    wv, ev, nv, pv, qv, dv, a0v, a1v, ov, eov, nov, gev, gnv, insem, smallsem, osem, rsem = refs[5:]
    me = lax.axis_index("field")
    small = [
        pltpu.make_async_copy(d_hbm, dv, smallsem.at[0]),
        pltpu.make_async_copy(a0_hbm, a0v, smallsem.at[1]),
        pltpu.make_async_copy(a1_hbm, a1v, smallsem.at[2]),
    ]
    for copy in small:
        copy.start()

    def inputs(x):
        pairs = [(p_hbm, pv), (w_hbm, wv), (e_hbm, ev), (n_hbm, nv)]
        copies = [
            pltpu.make_async_copy(src.at[:, x], dst.at[x], insem.at[i, x]) for i, (src, dst) in enumerate(pairs)
        ]
        for k in range(groups - 1):
            copies.append(pltpu.make_async_copy(q_hbm[k].at[:, x], qv.at[k, x], insem.at[4 + k, x]))
        return copies

    def outputs(x):
        copies = []
        for f in range(nf):
            for k in range(groups):
                g = lax.rem(me + k, groups) * nf
                copies.append(
                    pltpu.make_async_copy(
                        ov.at[x, f, k], node_hbm.at[f, pl.ds(g, nf), x], osem.at[f * groups + k, x]
                    )
                )
        if x < nx - 1:
            copies.append(pltpu.make_async_copy(eov.at[x], east_hbm.at[:, x], osem.at[nf * groups, x]))
        copies.append(
            pltpu.make_async_copy(
                nov.at[x], north_hbm.at[:, x, pl.ds(0, ny - 1)], osem.at[nf * groups + 1, x]
            )
        )
        return copies

    for x in range(nx):
        for copy in inputs(x):
            copy.start()
    for copy in small:
        copy.wait()
    off = jnp.where(iota((m, m), 0) == iota((m, m), 1), 0.0, 1.0).astype(BF)
    for copy in inputs(0):
        copy.wait()
    for x in range(nx):
        if x + 1 < nx:
            for copy in inputs(x + 1):
                copy.wait()
        for f in range(nf):
            for y in range(ny):
                a_row = a0v if y == 0 else a1v
                t = x * nf + f if y == 0 else (x * nf + f) * (ny - 1) + y - 1
                pt = jnp.transpose(pv[x, f, y])
                minus = -pt
                both = nn(minus, jnp.concatenate([wv[x, f, y] * off, ev[x, f, y]], axis=1))
                gn = nn(minus, nv[x, f, y]).astype(BF)
                ge = both[:, m:].astype(BF)
                if x + 1 < nx:
                    eov[x, f, y] = nn(ge, pv[x + 1, f, y]).astype(BF)
                else:
                    gev[f, y] = ge
                if y + 1 < ny:
                    nov[x, f, y] = nn(gn, pv[x, f, y + 1]).astype(BF)
                else:
                    gnv[x, f] = gn
                pt32 = pt.astype(F32)
                for k in range(groups):
                    g = lax.rem(me + k, groups) * nf
                    for j in range(nf):
                        row = dv[f, g + j, x, pl.ds(y, 1), :]
                        if k == 0 and j == f:
                            row = row + a_row[pl.ds(t, 1), :]
                            left = (pt32 * row + both[:, :m]).astype(BF)
                        else:
                            left = (pt32 * row).astype(BF)
                        right = pv[x, j, y] if k == 0 else qv[k - 1, x, j, y]
                        ov[x, f, k, j, y] = nn(left, right).astype(BF)
        for copy in outputs(x):
            copy.start()
    rims = [
        pltpu.make_async_copy(gev, ge_hbm, rsem.at[0]),
        pltpu.make_async_copy(gnv, gn_hbm, rsem.at[1]),
    ]
    for copy in rims:
        copy.start()
    for x in range(nx):
        for copy in outputs(x):
            copy.wait()
    for copy in rims:
        copy.wait()


def main_call(inner, east, north, interp, others, coupling, a0, a1):
    nf, nx, ny, m, _ = inner.shape
    groups = len(others) + 1
    tile = (m, m)
    out_shape = [
        jax.ShapeDtypeStruct((nf, groups * nf, nx, ny, m, m), BF),
        jax.ShapeDtypeStruct(inner.shape, BF),
        jax.ShapeDtypeStruct(inner.shape, BF),
        jax.ShapeDtypeStruct((nf, ny, m, m), BF),
        jax.ShapeDtypeStruct((nx, nf, m, m), BF),
    ]
    scratch = [pltpu.VMEM((nx, nf, ny) + tile, BF) for _ in range(4)] + [
        pltpu.VMEM((groups - 1, nx, nf, ny) + tile, BF),
        pltpu.VMEM(coupling.shape, F32),
        pltpu.VMEM(a0.shape, F32),
        pltpu.VMEM(a1.shape, F32),
        pltpu.VMEM((nx, nf, groups, nf, ny) + tile, BF),
        pltpu.VMEM((nx, nf, ny) + tile, BF),
        pltpu.VMEM((nx, nf, ny - 1) + tile, BF),
        pltpu.VMEM((nf, ny) + tile, BF),
        pltpu.VMEM((nx, nf) + tile, BF),
        pltpu.SemaphoreType.DMA((3 + groups, nx)),
        pltpu.SemaphoreType.DMA((3,)),
        pltpu.SemaphoreType.DMA((nf * groups + 2, nx)),
        pltpu.SemaphoreType.DMA((2,)),
    ]
    operands = [inner, east, north, interp, coupling, a0, a1] + list(others)

    def kernel(*refs):
        main_kernel((nf, nx, ny, m), groups, *refs)

    return pl.pallas_call(
        kernel,
        out_shape=out_shape,
        in_specs=[ANY] * len(operands),
        out_specs=[ANY] * len(out_shape),
        scratch_shapes=scratch,
        name="blocks",
    )(*operands)


def rim_kernel(shape, *refs):
    nf, nx, ny, m = shape
    half = m // 2
    east_hbm, north_hbm = refs[6:8]
    ge_hbm, gn_hbm, pe_hbm, z_hbm = refs[:4]
    gev, gnv, pev, zv, eov, nov, insem, osem = refs[8:]
    count = nf * nx
    rows = (z_hbm.shape[0] - count * half) // 3
    loads = [
        pltpu.make_async_copy(ge_hbm, gev, insem.at[0]),
        pltpu.make_async_copy(gn_hbm, gnv, insem.at[1]),
        pltpu.make_async_copy(pe_hbm, pev, insem.at[2]),
        pltpu.make_async_copy(z_hbm, zv, insem.at[3]),
    ]
    for copy in loads:
        copy.start()
    for copy in loads:
        copy.wait()
    stores = []
    for f in range(nf):
        for y in range(ny):
            eov[f, y] = nn(gev[f, y], pev[f, 0, y]).astype(BF)
    stores.append(pltpu.make_async_copy(eov, east_hbm.at[:, nx - 1], osem.at[nx]))
    stores[-1].start()
    base = count * half
    keys = zv[pl.ds(base, rows), :].astype(F32)
    cases = zv[pl.ds(base + rows, rows), :].astype(F32)
    flags = zv[pl.ds(base + 2 * rows, rows), :].astype(F32)
    for x in range(nx):
        for f in range(nf):
            t = x * nf + f
            few = cases[t : t + 1, :]
            few_half = jnp.broadcast_to(few, (half, m)).astype(BF)
            packed = zv[pl.ds(t * half, half), :]
            hot = one_hot(keys[t : t + 1, :], half)
            few_not = (1.0 - few_half.astype(F32)).astype(BF)
            first = packed * few_half + hot * few_not
            second = hot * few_half + packed * few_not
            g = gnv[x, f]
            mid = nt(g, first).astype(BF)
            rest = jnp.broadcast_to(flags[t : t + 1, :] * (1.0 - few), (m, m))
            nov[x, f] = (nn(mid, second) + g.astype(F32) * rest).astype(BF)
        stores.append(pltpu.make_async_copy(nov.at[x], north_hbm.at[:, x, ny - 1], osem.at[x]))
        stores[-1].start()
    for copy in stores:
        copy.wait()


def rim_call(ge, gn, pe, packed, east, north):
    nf, nx, ny, m, _ = east.shape
    operands = [ge, gn, pe, packed, east, north]
    tile = (m, m)
    scratch = [
        pltpu.VMEM(ge.shape, BF),
        pltpu.VMEM(gn.shape, BF),
        pltpu.VMEM(pe.shape, BF),
        pltpu.VMEM(packed.shape, BF),
        pltpu.VMEM((nf, ny) + tile, BF),
        pltpu.VMEM((nx, nf) + tile, BF),
        pltpu.SemaphoreType.DMA((4,)),
        pltpu.SemaphoreType.DMA((nx + 1,)),
    ]

    def kernel(*refs):
        rim_kernel((nf, nx, ny, m), *refs)

    return pl.pallas_call(
        kernel,
        out_shape=[jax.ShapeDtypeStruct(east.shape, BF), jax.ShapeDtypeStruct(north.shape, BF)],
        in_specs=[ANY] * len(operands),
        out_specs=[ANY] * 2,
        scratch_shapes=scratch,
        input_output_aliases={4: 0, 5: 1},
        name="rims",
    )(*operands)


def from_next(array, axis):
    devices = lax.axis_size(axis)
    return lax.ppermute(array, axis, [(i, i - 1) for i in range(1, devices)])


def body(inner_block, east_block, north_block, shift_diag, coupling, coarse_flags):
    ny = inner_block.shape[2]
    partial, a0, packed = interp_call(inner_block, shift_diag, coarse_flags, None, 0, 1)
    north_packed = from_next(packed, "sy")
    interp, a1 = interp_call(inner_block, shift_diag, coarse_flags, partial, 1, ny)
    groups = lax.axis_size("field")
    others = [
        lax.ppermute(interp, "field", [((i + k) % groups, i) for i in range(groups)]) for k in range(1, groups)
    ]
    east_interp = from_next(interp[:, :1], "sx")
    coarse_node, coarse_east, coarse_north, ge, gn = main_call(
        inner_block, east_block, north_block, interp, others, coupling, a0, a1
    )
    coarse_east, coarse_north = rim_call(ge, gn, east_interp, north_packed, coarse_east, coarse_north)
    return (coarse_node, coarse_east, coarse_north)


def solution(mesh):
    in_specs = (
        P("field", "sx", "sy", None, None),
        P("field", "sx", "sy", None, None),
        P("field", "sx", "sy", None, None),
        P("field", "sx", "sy", None),
        P("field", None, "sx", "sy", None),
        P("field", "sx", "sy", None),
    )
    out_specs = (
        P("field", None, "sx", "sy", None, None),
        P("field", "sx", "sy", None, None),
        P("field", "sx", "sy", None, None),
    )
    return jax.shard_map(body, mesh=mesh, in_specs=in_specs, out_specs=out_specs, check_vma=False)
```
